32 devices in a mesh: col: 32 (over z, y, x, core).
Axes of the slice: x: 2, y: 2, z: 4, core: 2. Of those that a mesh axis runs over, the one named last changes fastest.
Arguments:
- a_band: float32 [1536, 24576], P(None, 'col'), may hold values from -6 to 6
- b_band: float32 [1536, 24576], P(None, 'col'), may hold values from -6 to 6
- z_band: float32 [1536, 24576], P(None, 'col'), may hold values from -6 to 6
- stacked_left_factors: float32 [1536, 384], P('col'), may hold values from -0.3125 to 0.3125
- right_factors: float32 [1536, 384], P('col'), may hold values from -0.3125 to 0.3125
- starts: int32 [4], replicated, may hold values from 512 to 23680, as said below
Outputs:
- a_out: float32 [1536, 24576], P(None, 'col')
- b_out: float32 [1536, 24576], P(None, 'col')
- z_out: float32 [1536, 24576], P(None, 'col')
The draws below stay inside these ranges and needn't reach their ends.
Inputs may be any that keep to these rules, and one draw needn't show every extreme that they name: `starts`: Increasing; each a multiple of 128; each window's columns s to s + 383 cross exactly one border between slabs of 768 columns, and different windows cross different borders.
All inputs are finite; a program needn't handle non-finite values.
Results may differ from the reference program's by a relative error of at most 0.0001.
Values sent between devices are 32-bit elements; how exact they have to be, the bound alone decides.
A program may use at most 448 MiB of HBM per device.

```python
import jax
import jax.numpy as jnp
from jax import lax

W = 384
ALIGN = 128
WIN = 4
COLS = 768
ROWS = 1536
N = 24576
N_COL = 32


def draw_starts(key, part):
    order_key = jax.random.fold_in(key, 11)
    shift_key = jax.random.fold_in(key, 12)
    borders = jnp.arange(1, N_COL, dtype=jnp.int32)
    scores = jax.random.permutation(order_key, N_COL - 1).astype(jnp.int32)
    forced = (borders == 1) | (borders == N_COL // 2) | (borders == N_COL - 1)
    scores = scores + forced.astype(jnp.int32) * N_COL
    picked = lax.top_k(scores, WIN)[1].astype(jnp.int32)
    chosen = jnp.sort(picked + 1).astype(jnp.int32)
    shifts = jax.random.randint(shift_key, (WIN,), 1, W // ALIGN).astype(jnp.int32)
    window_ids = lax.iota(jnp.int32, WIN)
    shifts = jnp.where(window_ids == 0, W // ALIGN - 1, shifts)
    shifts = jnp.where(window_ids == WIN - 1, 1, shifts).astype(jnp.int32)
    return (chosen * COLS - ALIGN * shifts).astype(jnp.int32)


def levels(key, dims, pieces, low, largest):
    factor_of = 1.0
    for axis_at, shards_of in pieces:
        draws = jax.random.uniform(jax.random.fold_in(jax.random.fold_in(key, 6), axis_at), (shards_of,), jnp.float32, low / len(pieces), largest / len(pieces))
        factor_of = factor_of * jnp.repeat(jnp.exp(draws), dims[axis_at] // shards_of).reshape((-1,) + (1,) * (len(dims) - 1 - axis_at))
    return factor_of


def centred(own_key, shape, spread, reach, cuts=(), held_as=jnp.bfloat16):
    entries = spread * jax.random.normal(own_key, shape, jnp.float32)
    if cuts:
        entries = entries * levels(own_key, shape, cuts, -0.22, 0.18)
    return jnp.clip(entries, -reach, reach).astype(held_as)


def setup_inputs(seed: int = 0) -> dict:
    streams_of = jax.random.split(jax.random.key(seed), 7)
    return {
        "a_band": centred(streams_of[0], (ROWS, N), 1.0, 6.0, ((1, 32),), jnp.float32),
        "b_band": centred(streams_of[1], (ROWS, N), 1.0, 6.0, ((1, 32),), jnp.float32),
        "z_band": centred(streams_of[2], (ROWS, N), 1.0, 6.0, ((1, 32),), jnp.float32),
        "stacked_left_factors": centred(streams_of[3], (WIN * W, W), W ** -0.5, 0.3125, ((0, 32),), jnp.float32),
        "right_factors": centred(streams_of[4], (WIN * W, W), W ** -0.5, 0.3125, ((0, 32),), jnp.float32),
        "starts": draw_starts(jax.random.fold_in(streams_of[6], 71), 0),
    }


HIGHEST_PRECISION = lax.Precision.HIGHEST


def reference(a_band, b_band, z_band, stacked_left_factors, right_factors, starts):
    width = stacked_left_factors.shape[1]
    count = starts.shape[0]
    lefts = stacked_left_factors.reshape(count, width, width)
    right_factor_list = right_factors.reshape(count, width, width)
    column_ids = lax.iota(jnp.int32, a_band.shape[1])
    row_ids = lax.iota(jnp.int32, a_band.shape[0])
    bands = [a_band, b_band]
    for bulge_window in range(count):
        start = starts[bulge_window].astype(jnp.int32)
        keep = (column_ids >= start)[None, :]
        low = bulge_window * width
        for which in range(2):
            offdiag_panel = bands[which][low:low + width]
            rotated_panel = jnp.dot(lefts[bulge_window].T, offdiag_panel, precision=HIGHEST_PRECISION, preferred_element_type=jnp.float32)
            bands[which] = bands[which].at[low:low + width].set(jnp.where(keep, rotated_panel, offdiag_panel))
    bands.append(z_band)
    for bulge_window in range(count):
        start = starts[bulge_window].astype(jnp.int32)
        above = (row_ids < (bulge_window + 1) * width)[:, None]
        for which in range(3):
            offdiag_panel = lax.dynamic_slice_in_dim(bands[which], start, width, 1)
            rotated_panel = jnp.dot(offdiag_panel, right_factor_list[bulge_window], precision=HIGHEST_PRECISION, preferred_element_type=jnp.float32)
            if which < 2:
                rotated_panel = jnp.where(above, rotated_panel, offdiag_panel)
            bands[which] = lax.dynamic_update_slice_in_dim(bands[which], rotated_panel, start, 1)
    return (bands[0], bands[1], bands[2])
```

```python
import functools

import jax
import jax.numpy as jnp
from jax import lax
from jax.experimental import pallas as pl
from jax.experimental.pallas import tpu as pltpu
from jax.sharding import PartitionSpec as P

ALIGN = 128
F32 = jnp.float32
BF16 = jnp.bfloat16
VMEM_LIMIT = 60 * 1024 * 1024


def split(x):
    high = x.astype(BF16)
    return high, (x - high.astype(F32)).astype(BF16)


def mm(x, w):
    rows = x.shape[0]
    xh, xl = split(x)
    wh, wl = split(w)
    both = jnp.dot(jnp.concatenate([xh, xl], axis=0), wh, preferred_element_type=F32)
    return both[:rows] + (both[rows:] + jnp.dot(xh, wl, preferred_element_type=F32))


def borders(info, count, width, cols):
    first = info[count]
    last = first + cols
    left = (jnp.bool_(False), jnp.int32(0), jnp.int32(0))
    right = left
    for k in range(count):
        s = info[k]
        at_left = (s < first) & (first < s + width)
        at_right = (s < last) & (last < s + width)
        left = (
            left[0] | at_left,
            jnp.where(at_left, k, left[1]),
            jnp.where(at_left, s + width - first, left[2]),
        )
        right = (
            right[0] | at_right,
            jnp.where(at_right, k, right[1]),
            jnp.where(at_right, last - s, right[2]),
        )
    return first, left, right


def prep_kernel(count, width, cols, info, al, ar, bl, br, zl, zr, rights, down, up):
    wide = width - ALIGN
    _, left, right = borders(info, count, width, cols)
    for i, (lo, hi) in enumerate(((al, ar), (bl, br), (zl, zr))):
        full_left = left[0] & (left[2] == wide)
        full_right = right[0] & (right[2] == wide)

        @pl.when(full_left)
        def _():
            down[i] = mm(lo[...], rights[left[1], width - wide : width, 0:ALIGN])

        @pl.when(jnp.logical_not(full_left))
        def _():
            down[i] = lo[:, 0:ALIGN]

        @pl.when(full_right)
        def _():
            up[i] = mm(hi[...], rights[right[1], 0:wide, width - ALIGN : width])

        @pl.when(jnp.logical_not(full_right))
        def _():
            up[i] = hi[:, wide - ALIGN : wide]


def main_kernel(count, width, cols, info, a, b, z, left_factor, rights, a_out, b_out, z_out):
    wide = width - ALIGN
    j = pl.program_id(0)
    first, left, right = borders(info, count, width, cols)
    threshold = info[j] - first

    @pl.when(threshold < cols)
    def _():
        turned = left_factor[...].T
        keep = lax.broadcasted_iota(jnp.int32, (width, cols), 1) >= threshold
        for src, dst in ((a, a_out), (b, b_out)):
            x = src[...]
            dst[...] = jnp.where(keep, mm(turned, x), x)

    @pl.when(threshold >= cols)
    def _():
        a_out[...] = a[...]
        b_out[...] = b[...]

    z_out[...] = z[...]
    for dst, always in ((a_out, False), (b_out, False), (z_out, True)):
        on_left = left[0] if always else left[0] & (j <= left[1])
        on_right = right[0] if always else right[0] & (j <= right[1])

        @pl.when(on_left & (left[2] == wide))
        def _():
            dst[:, 0:wide] = mm(dst[:, 0:wide], rights[left[1], width - wide : width, width - wide : width])

        @pl.when(on_left & (left[2] == ALIGN))
        def _():
            dst[:, 0:ALIGN] = mm(dst[:, 0:ALIGN], rights[left[1], width - ALIGN : width, width - ALIGN : width])

        @pl.when(on_right & (right[2] == wide))
        def _():
            dst[:, cols - wide : cols] = mm(dst[:, cols - wide : cols], rights[right[1], 0:wide, 0:wide])

        @pl.when(on_right & (right[2] == ALIGN))
        def _():
            dst[:, cols - ALIGN : cols] = mm(dst[:, cols - ALIGN : cols], rights[right[1], 0:ALIGN, 0:ALIGN])


def finish_kernel(count, width, cols, info, a, b, z, from_left, from_right, left_factor, rights, a_out, b_out, z_out):
    wide = width - ALIGN
    j = pl.program_id(0)
    side = pl.program_id(1)
    _, left, right = borders(info, count, width, cols)
    for src, dst in ((a, a_out), (b, b_out), (z, z_out)):
        dst[...] = src[...]

    def add(received, at, rows_of, near, far, window):
        present, k, here = window
        for i, dst in enumerate((a_out, b_out, z_out)):
            wanted = present & (side == at)
            if i < 2:
                wanted = wanted & (j <= k)

            @pl.when(wanted)
            def _():
                g = received[i]
                if i < 2:
                    g = mm(left_factor[...].T, g)

                @pl.when(here == wide)
                def _():
                    dst[...] = dst[...] + mm(g, rights[k, rows_of : rows_of + ALIGN, far : far + wide])

                @pl.when(here == ALIGN)
                def _():
                    dst[:, near : near + ALIGN] = dst[:, near : near + ALIGN] + g

    add(from_left, 0, 0, 0, width - wide, left)
    add(from_right, 1, width - ALIGN, wide - ALIGN, 0, right)


def gathered(x, n):
    return lax.all_gather(x, "col", axis=0, tiled=True)


def local(n, a_band, b_band, z_band, stacked_left_factors, right_factors, starts):
    width = stacked_left_factors.shape[1]
    count = starts.shape[0]
    rows, cols = a_band.shape
    wide = width - ALIGN
    lefts = gathered(stacked_left_factors, n).reshape(count, width, width)
    rights = gathered(right_factors, n).reshape(count, width, width)
    first = (lax.axis_index("col") * cols).astype(jnp.int32)
    info = jnp.concatenate([starts, first[None]])
    far = cols // wide - 1
    params = pltpu.CompilerParams(vmem_limit_bytes=VMEM_LIMIT)
    all_rights = pl.BlockSpec((count, width, width), lambda *_: (0, 0, 0), pipeline_mode=pl.Buffered(1))
    strip = jax.ShapeDtypeStruct((3, rows, ALIGN), F32)
    low = pl.BlockSpec((width, wide), lambda j, s: (j, 0))
    high = pl.BlockSpec((width, wide), lambda j, s: (j, far))
    strip_spec = pl.BlockSpec((3, width, ALIGN), lambda j, *_: (0, j, 0))
    down, up = pl.pallas_call(
        functools.partial(prep_kernel, count, width, cols),
        out_shape=(strip, strip),
        grid_spec=pltpu.PrefetchScalarGridSpec(
            num_scalar_prefetch=1,
            grid=(count,),
            in_specs=[low, high, low, high, low, high, all_rights],
            out_specs=[strip_spec, strip_spec],
        ),
        compiler_params=params,
        name="prep",
    )(info, a_band, a_band, b_band, b_band, z_band, z_band, rights)
    from_left = lax.ppermute(up, "col", [(i, i + 1) for i in range(n - 1)])
    from_right = lax.ppermute(down, "col", [(i + 1, i) for i in range(n - 1)])
    whole = jax.ShapeDtypeStruct((rows, cols), F32)
    slab = pl.BlockSpec((width, cols), lambda j, s: (j, 0))
    one_left = pl.BlockSpec((None, width, width), lambda j, *_: (j, 0, 0))
    a_mid, b_mid, z_mid = pl.pallas_call(
        functools.partial(main_kernel, count, width, cols),
        out_shape=(whole, whole, whole),
        grid_spec=pltpu.PrefetchScalarGridSpec(
            num_scalar_prefetch=1,
            grid=(count,),
            in_specs=[slab, slab, slab, one_left, all_rights],
            out_specs=[slab, slab, slab],
        ),
        compiler_params=params,
        cost_estimate=pl.CostEstimate(
            flops=20 * rows * cols * width, bytes_accessed=24 * rows * cols, transcendentals=0
        ),
        name="main",
    )(info, a_band, b_band, z_band, lefts, rights)
    edge = pl.BlockSpec((width, wide), lambda j, e, s: (j, e * far))
    return pl.pallas_call(
        functools.partial(finish_kernel, count, width, cols),
        out_shape=(whole, whole, whole),
        grid_spec=pltpu.PrefetchScalarGridSpec(
            num_scalar_prefetch=1,
            grid=(count, 2),
            in_specs=[edge, edge, edge, strip_spec, strip_spec, one_left, all_rights],
            out_specs=[edge, edge, edge],
        ),
        input_output_aliases={1: 0, 2: 1, 3: 2},
        compiler_params=params,
        name="finish",
    )(info, a_mid, b_mid, z_mid, from_left, from_right, lefts, rights)


def solution(mesh):
    placed = (P(None, "col"), P(None, "col"), P(None, "col"), P("col", None), P("col", None), P())
    return jax.shard_map(
        functools.partial(local, mesh.shape["col"]),
        mesh=mesh,
        in_specs=placed,
        out_specs=(P(None, "col"), P(None, "col"), P(None, "col")),
        check_vma=False,
    )
```

```python
import functools

import jax
import jax.numpy as jnp
from jax import lax
from jax.experimental import pallas as pl
from jax.experimental.pallas import tpu as pltpu
from jax.sharding import PartitionSpec as P

ALIGN = 128
CORES = 2
PLANE = 4
F32 = jnp.float32
BF16 = jnp.bfloat16
VMEM_LIMIT = 60 * 1024 * 1024


def split(x):
    high = x.astype(BF16)
    return high, (x - high.astype(F32)).astype(BF16)


def mm(x, w):
    rows = x.shape[0]
    xh, xl = split(x)
    wh, wl = split(w)
    both = jnp.dot(jnp.concatenate([xh, xl], axis=0), wh, preferred_element_type=F32)
    return both[:rows] + (both[rows:] + jnp.dot(xh, wl, preferred_element_type=F32))


def borders(info, count, width, cols):
    first = info[count]
    last = first + cols
    left = (jnp.bool_(False), jnp.int32(0), jnp.int32(0))
    right = left
    for k in range(count):
        s = info[k]
        at_left = (s < first) & (first < s + width)
        at_right = (s < last) & (last < s + width)
        left = (
            left[0] | at_left,
            jnp.where(at_left, k, left[1]),
            jnp.where(at_left, s + width - first, left[2]),
        )
        right = (
            right[0] | at_right,
            jnp.where(at_right, k, right[1]),
            jnp.where(at_right, last - s, right[2]),
        )
    return first, left, right


def prep_kernel(count, width, cols, info, al, ar, bl, br, zl, zr, rights, down, up):
    wide = width - ALIGN
    _, left, right = borders(info, count, width, cols)
    for i, (lo, hi) in enumerate(((al, ar), (bl, br), (zl, zr))):
        full_left = left[0] & (left[2] == wide)
        full_right = right[0] & (right[2] == wide)

        @pl.when(full_left)
        def _():
            down[i] = mm(lo[...], rights[left[1], width - wide : width, 0:ALIGN])

        @pl.when(jnp.logical_not(full_left))
        def _():
            down[i] = lo[:, 0:ALIGN]

        @pl.when(full_right)
        def _():
            up[i] = mm(hi[...], rights[right[1], 0:wide, width - ALIGN : width])

        @pl.when(jnp.logical_not(full_right))
        def _():
            up[i] = hi[:, wide - ALIGN : wide]


def main_kernel(count, width, cols, info, a, b, z, left_factor, rights, a_out, b_out, z_out):
    wide = width - ALIGN
    j = pl.program_id(0)
    first, left, right = borders(info, count, width, cols)
    threshold = info[j] - first

    @pl.when(threshold < cols)
    def _():
        turned = left_factor[...].T
        keep = lax.broadcasted_iota(jnp.int32, (width, cols), 1) >= threshold
        for src, dst in ((a, a_out), (b, b_out)):
            x = src[...]
            dst[...] = jnp.where(keep, mm(turned, x), x)

    @pl.when(threshold >= cols)
    def _():
        a_out[...] = a[...]
        b_out[...] = b[...]

    z_out[...] = z[...]
    for dst, always in ((a_out, False), (b_out, False), (z_out, True)):
        on_left = left[0] if always else left[0] & (j <= left[1])
        on_right = right[0] if always else right[0] & (j <= right[1])

        @pl.when(on_left & (left[2] == wide))
        def _():
            dst[:, 0:wide] = mm(dst[:, 0:wide], rights[left[1], width - wide : width, width - wide : width])

        @pl.when(on_left & (left[2] == ALIGN))
        def _():
            dst[:, 0:ALIGN] = mm(dst[:, 0:ALIGN], rights[left[1], width - ALIGN : width, width - ALIGN : width])

        @pl.when(on_right & (right[2] == wide))
        def _():
            dst[:, cols - wide : cols] = mm(dst[:, cols - wide : cols], rights[right[1], 0:wide, 0:wide])

        @pl.when(on_right & (right[2] == ALIGN))
        def _():
            dst[:, cols - ALIGN : cols] = mm(dst[:, cols - ALIGN : cols], rights[right[1], 0:ALIGN, 0:ALIGN])


def finish_kernel(count, width, cols, info, a, b, z, from_left, from_right, left_factor, rights, a_out, b_out, z_out):
    wide = width - ALIGN
    j = pl.program_id(0)
    side = pl.program_id(1)
    _, left, right = borders(info, count, width, cols)
    for src, dst in ((a, a_out), (b, b_out), (z, z_out)):
        dst[...] = src[...]

    def add(received, at, rows_of, near, far, window):
        present, k, here = window
        for i, dst in enumerate((a_out, b_out, z_out)):
            wanted = present & (side == at)
            if i < 2:
                wanted = wanted & (j <= k)

            @pl.when(wanted)
            def _():
                g = received[i]
                if i < 2:
                    g = mm(left_factor[...].T, g)

                @pl.when(here == wide)
                def _():
                    dst[...] = dst[...] + mm(g, rights[k, rows_of : rows_of + ALIGN, far : far + wide])

                @pl.when(here == ALIGN)
                def _():
                    dst[:, near : near + ALIGN] = dst[:, near : near + ALIGN] + g

    add(from_left, 0, 0, 0, width - wide, left)
    add(from_right, 1, width - ALIGN, wide - ALIGN, 0, right)


def gather_kernel(n, rights, lefts, all_rights, all_lefts, own_sem, out_sems, plane_sems, core_sems, recv_sems):
    me = lax.axis_index("col")
    core = lax.rem(me, CORES)
    chip = me // CORES
    place = lax.rem(chip, PLANE)
    outer = chip // PLANE
    outers = n // (CORES * PLANE)
    pair = ((rights, all_rights), (lefts, all_lefts))

    def device(o, p, c):
        return (lax.rem(o, outers) * PLANE + lax.rem(p, PLANE)) * CORES + c

    far = [device(outer + d, place, core) for d in range(1, outers)]
    near = [device(outer, place + q, core) for q in range(1, PLANE)]
    twin = device(outer, place, 1 - core)

    barrier = pltpu.get_barrier_semaphore()
    for peer in far + near + [twin]:
        pl.semaphore_signal(barrier, inc=1, device_id=(peer,), device_id_type=pl.DeviceIdType.MESH)
    pl.semaphore_wait(barrier, len(far) + len(near) + 1)

    started = []

    def send(which, source, piece, send_sem, target):
        copy = pltpu.make_async_remote_copy(
            src_ref=source,
            dst_ref=pair[which][1].at[piece],
            send_sem=send_sem,
            recv_sem=recv_sems.at[which, piece],
            device_id=(target,),
            device_id_type=pl.DeviceIdType.MESH,
        )
        copy.start()
        started.append(copy)

    def arrived(which, piece):
        here = pair[which][1].at[piece]
        pltpu.make_async_copy(here, here, recv_sems.at[which, piece]).wait()

    def spread(which, source, piece, d):
        for q in range(1, PLANE):
            send(which, source, piece, plane_sems.at[which, d, q - 1], near[q - 1])
        send(which, source, piece, core_sems.at[which, d, 0], twin)

    own = []
    for which, (mine, everyone) in enumerate(pair):
        for d in range(1, outers):
            send(which, mine, me, out_sems.at[which, d - 1], far[d - 1])
        spread(which, mine, me, 0)
        own.append(pltpu.make_async_copy(mine, everyone.at[me], own_sem.at[which]))
        own[-1].start()
    for which, (_, everyone) in enumerate(pair):
        for d in range(1, outers):
            piece = device(outer + outers - d, place, core)
            arrived(which, piece)
            spread(which, everyone.at[piece], piece, d)
    for which, (_, everyone) in enumerate(pair):
        for d in range(outers):
            for q in range(1, PLANE):
                piece = device(outer + outers - d, place + PLANE - q, core)
                arrived(which, piece)
                send(which, everyone.at[piece], piece, core_sems.at[which, d, q], twin)
    for which in range(2):
        for d in range(outers):
            for q in range(PLANE):
                arrived(which, device(outer + outers - d, place + PLANE - q, 1 - core))
    for copy in started:
        copy.wait_send()
    for copy in own:
        copy.wait()


def gathered(rights, lefts, n):
    pieces = jax.ShapeDtypeStruct((n,) + rights.shape, F32)
    outers = n // (CORES * PLANE)
    vmem = pl.BlockSpec(memory_space=pltpu.VMEM)
    anywhere = pl.BlockSpec(memory_space=pl.ANY)
    dma = pltpu.SemaphoreType.DMA
    return pl.pallas_call(
        functools.partial(gather_kernel, n),
        out_shape=(pieces, pieces),
        in_specs=[vmem, vmem],
        out_specs=(anywhere, anywhere),
        scratch_shapes=[
            dma((2,)),
            dma((2, max(outers - 1, 1))),
            dma((2, outers, PLANE - 1)),
            dma((2, outers, PLANE)),
            dma((2, n)),
        ],
        compiler_params=pltpu.CompilerParams(collective_id=0, has_side_effects=True),
        name="gather",
    )(rights, lefts)


def local(n, a_band, b_band, z_band, stacked_left_factors, right_factors, starts):
    width = stacked_left_factors.shape[1]
    count = starts.shape[0]
    rows, cols = a_band.shape
    wide = width - ALIGN
    rights, lefts = gathered(right_factors, stacked_left_factors, n)
    rights = rights.reshape(count, width, width)
    lefts = lefts.reshape(count, width, width)
    first = (lax.axis_index("col") * cols).astype(jnp.int32)
    info = jnp.concatenate([starts, first[None]])
    far = cols // wide - 1
    params = pltpu.CompilerParams(vmem_limit_bytes=VMEM_LIMIT)
    all_rights = pl.BlockSpec((count, width, width), lambda *_: (0, 0, 0), pipeline_mode=pl.Buffered(1))
    strip = jax.ShapeDtypeStruct((3, rows, ALIGN), F32)
    low = pl.BlockSpec((width, wide), lambda j, s: (j, 0))
    high = pl.BlockSpec((width, wide), lambda j, s: (j, far))
    strip_spec = pl.BlockSpec((3, width, ALIGN), lambda j, *_: (0, j, 0))
    down, up = pl.pallas_call(
        functools.partial(prep_kernel, count, width, cols),
        out_shape=(strip, strip),
        grid_spec=pltpu.PrefetchScalarGridSpec(
            num_scalar_prefetch=1,
            grid=(count,),
            in_specs=[low, high, low, high, low, high, all_rights],
            out_specs=[strip_spec, strip_spec],
        ),
        compiler_params=params,
        name="prep",
    )(info, a_band, a_band, b_band, b_band, z_band, z_band, rights)
    from_left = lax.ppermute(up, "col", [(i, i + 1) for i in range(n - 1)])
    from_right = lax.ppermute(down, "col", [(i + 1, i) for i in range(n - 1)])
    whole = jax.ShapeDtypeStruct((rows, cols), F32)
    slab = pl.BlockSpec((width, cols), lambda j, s: (j, 0))
    one_left = pl.BlockSpec((None, width, width), lambda j, *_: (j, 0, 0))
    a_mid, b_mid, z_mid = pl.pallas_call(
        functools.partial(main_kernel, count, width, cols),
        out_shape=(whole, whole, whole),
        grid_spec=pltpu.PrefetchScalarGridSpec(
            num_scalar_prefetch=1,
            grid=(count,),
            in_specs=[slab, slab, slab, one_left, all_rights],
            out_specs=[slab, slab, slab],
        ),
        compiler_params=params,
        cost_estimate=pl.CostEstimate(
            flops=20 * rows * cols * width, bytes_accessed=24 * rows * cols, transcendentals=0
        ),
        name="main",
    )(info, a_band, b_band, z_band, lefts, rights)
    edge = pl.BlockSpec((width, wide), lambda j, e, s: (j, e * far))
    return pl.pallas_call(
        functools.partial(finish_kernel, count, width, cols),
        out_shape=(whole, whole, whole),
        grid_spec=pltpu.PrefetchScalarGridSpec(
            num_scalar_prefetch=1,
            grid=(count, 2),
            in_specs=[edge, edge, edge, strip_spec, strip_spec, one_left, all_rights],
            out_specs=[edge, edge, edge],
        ),
        input_output_aliases={1: 0, 2: 1, 3: 2},
        compiler_params=params,
        name="finish",
    )(info, a_mid, b_mid, z_mid, from_left, from_right, lefts, rights)


def solution(mesh):
    placed = (P(None, "col"), P(None, "col"), P(None, "col"), P("col", None), P("col", None), P())
    return jax.shard_map(
        functools.partial(local, mesh.shape["col"]),
        mesh=mesh,
        in_specs=placed,
        out_specs=(P(None, "col"), P(None, "col"), P(None, "col")),
        check_vma=False,
    )
```

```python
import functools

import jax
import jax.numpy as jnp
from jax import lax
from jax.experimental import pallas as pl
from jax.experimental.pallas import tpu as pltpu
from jax.sharding import PartitionSpec as P

ALIGN = 128
CORES = 2
PLANE = 4
F32 = jnp.float32
BF16 = jnp.bfloat16
VMEM_LIMIT = 60 * 1024 * 1024


def split(x):
    high = x.astype(BF16)
    return high, (x - high.astype(F32)).astype(BF16)


def mm(x, w):
    rows = x.shape[0]
    xh, xl = split(x)
    wh, wl = split(w)
    both = jnp.dot(jnp.concatenate([xh, xl], axis=0), wh, preferred_element_type=F32)
    return both[:rows] + (both[rows:] + jnp.dot(xh, wl, preferred_element_type=F32))


def borders(info, count, width, cols):
    first = info[count]
    last = first + cols
    left = (jnp.bool_(False), jnp.int32(0), jnp.int32(0))
    right = left
    for k in range(count):
        s = info[k]
        at_left = (s < first) & (first < s + width)
        at_right = (s < last) & (last < s + width)
        left = (
            left[0] | at_left,
            jnp.where(at_left, k, left[1]),
            jnp.where(at_left, s + width - first, left[2]),
        )
        right = (
            right[0] | at_right,
            jnp.where(at_right, k, right[1]),
            jnp.where(at_right, last - s, right[2]),
        )
    return first, left, right


def prep_kernel(count, width, cols, info, al, ar, bl, br, zl, zr, rights, down, up):
    wide = width - ALIGN
    _, left, right = borders(info, count, width, cols)
    for i, (lo, hi) in enumerate(((al, ar), (bl, br), (zl, zr))):
        full_left = left[0] & (left[2] == wide)
        full_right = right[0] & (right[2] == wide)

        @pl.when(full_left)
        def _():
            down[i] = mm(lo[...], rights[left[1], width - wide : width, 0:ALIGN])

        @pl.when(jnp.logical_not(full_left))
        def _():
            down[i] = lo[:, 0:ALIGN]

        @pl.when(full_right)
        def _():
            up[i] = mm(hi[...], rights[right[1], 0:wide, width - ALIGN : width])

        @pl.when(jnp.logical_not(full_right))
        def _():
            up[i] = hi[:, wide - ALIGN : wide]


def main_kernel(count, width, cols, info, a, b, z, left_factor, rights, a_out, b_out, z_out):
    wide = width - ALIGN
    j = pl.program_id(0)
    first, left, right = borders(info, count, width, cols)
    threshold = info[j] - first

    @pl.when(threshold < cols)
    def _():
        turned = left_factor[...].T
        keep = lax.broadcasted_iota(jnp.int32, (width, cols), 1) >= threshold
        for src, dst in ((a, a_out), (b, b_out)):
            x = src[...]
            dst[...] = jnp.where(keep, mm(turned, x), x)

    @pl.when(threshold >= cols)
    def _():
        a_out[...] = a[...]
        b_out[...] = b[...]

    z_out[...] = z[...]
    for dst, always in ((a_out, False), (b_out, False), (z_out, True)):
        on_left = left[0] if always else left[0] & (j <= left[1])
        on_right = right[0] if always else right[0] & (j <= right[1])

        @pl.when(on_left & (left[2] == wide))
        def _():
            dst[:, 0:wide] = mm(dst[:, 0:wide], rights[left[1], width - wide : width, width - wide : width])

        @pl.when(on_left & (left[2] == ALIGN))
        def _():
            dst[:, 0:ALIGN] = mm(dst[:, 0:ALIGN], rights[left[1], width - ALIGN : width, width - ALIGN : width])

        @pl.when(on_right & (right[2] == wide))
        def _():
            dst[:, cols - wide : cols] = mm(dst[:, cols - wide : cols], rights[right[1], 0:wide, 0:wide])

        @pl.when(on_right & (right[2] == ALIGN))
        def _():
            dst[:, cols - ALIGN : cols] = mm(dst[:, cols - ALIGN : cols], rights[right[1], 0:ALIGN, 0:ALIGN])


def edge_of(count, width, cols, upto, step, info):
    _, left, right = borders(info, count, width, cols)
    side = step // count
    j = lax.rem(step, count)
    low_last, high_last = (left[1], right[1]) if upto else (count - 1, count - 1)
    low = jnp.where(left[0], jnp.where(side == 0, jnp.minimum(j, low_last), low_last), 0)
    high = jnp.where(side == 0, 0, jnp.minimum(j, high_last))
    at_high = right[0] & ((side == 1) | jnp.logical_not(left[0]))
    return jnp.where(at_high, high, low), at_high.astype(jnp.int32)


def finish_kernel(count, width, cols, info, a, b, z, from_left, from_right, left_factor, rights, a_out, b_out, z_out):
    wide = width - ALIGN
    step = pl.program_id(0)
    side = step // count
    j = lax.rem(step, count)
    _, left, right = borders(info, count, width, cols)
    for upto, group in ((True, ((a, a_out), (b, b_out))), (False, ((z, z_out),))):
        now = edge_of(count, width, cols, upto, step, info)
        then = edge_of(count, width, cols, upto, jnp.maximum(step - 1, 0), info)

        @pl.when((step == 0) | (now[0] != then[0]) | (now[1] != then[1]))
        def _():
            for src, dst in group:
                dst[...] = src[...]

    def add(received, at, rows_of, near, far, window):
        present, k, here = window
        for i, dst in enumerate((a_out, b_out, z_out)):
            wanted = present & (side == at)
            if i < 2:
                wanted = wanted & (j <= k)

            @pl.when(wanted)
            def _():
                g = received[i]
                if i < 2:
                    g = mm(left_factor[...].T, g)

                @pl.when(here == wide)
                def _():
                    dst[...] = dst[...] + mm(g, rights[k, rows_of : rows_of + ALIGN, far : far + wide])

                @pl.when(here == ALIGN)
                def _():
                    dst[:, near : near + ALIGN] = dst[:, near : near + ALIGN] + g

    add(from_left, 0, 0, 0, width - wide, left)
    add(from_right, 1, width - ALIGN, wide - ALIGN, 0, right)


def gather_kernel(n, rights, lefts, all_rights, all_lefts, own_sem, out_sems, plane_sems, core_sems, recv_sems):
    me = lax.axis_index("col")
    core = lax.rem(me, CORES)
    chip = me // CORES
    place = lax.rem(chip, PLANE)
    outer = chip // PLANE
    outers = n // (CORES * PLANE)
    pair = ((rights, all_rights), (lefts, all_lefts))

    def device(o, p, c):
        return (lax.rem(o, outers) * PLANE + lax.rem(p, PLANE)) * CORES + c

    far = [device(outer + d, place, core) for d in range(1, outers)]
    near = [device(outer, place + q, core) for q in range(1, PLANE)]
    twin = device(outer, place, 1 - core)

    barrier = pltpu.get_barrier_semaphore()
    for peer in far + near + [twin]:
        pl.semaphore_signal(barrier, inc=1, device_id=(peer,), device_id_type=pl.DeviceIdType.MESH)
    pl.semaphore_wait(barrier, len(far) + len(near) + 1)

    started = []

    def send(which, source, piece, send_sem, target):
        copy = pltpu.make_async_remote_copy(
            src_ref=source,
            dst_ref=pair[which][1].at[piece],
            send_sem=send_sem,
            recv_sem=recv_sems.at[which, piece],
            device_id=(target,),
            device_id_type=pl.DeviceIdType.MESH,
        )
        copy.start()
        started.append(copy)

    def arrived(which, piece):
        here = pair[which][1].at[piece]
        pltpu.make_async_copy(here, here, recv_sems.at[which, piece]).wait()

    def spread(which, source, piece, d):
        for q in range(1, PLANE):
            send(which, source, piece, plane_sems.at[which, d, q - 1], near[q - 1])
        send(which, source, piece, core_sems.at[which, d, 0], twin)

    own = []
    for which, (mine, everyone) in enumerate(pair):
        for d in range(1, outers):
            send(which, mine, me, out_sems.at[which, d - 1], far[d - 1])
        spread(which, mine, me, 0)
        own.append(pltpu.make_async_copy(mine, everyone.at[me], own_sem.at[which]))
        own[-1].start()
    for which, (_, everyone) in enumerate(pair):
        for d in range(1, outers):
            piece = device(outer + outers - d, place, core)
            arrived(which, piece)
            spread(which, everyone.at[piece], piece, d)
    for which, (_, everyone) in enumerate(pair):
        for d in range(outers):
            for q in range(1, PLANE):
                piece = device(outer + outers - d, place + PLANE - q, core)
                arrived(which, piece)
                send(which, everyone.at[piece], piece, core_sems.at[which, d, q], twin)
    for which in range(2):
        for d in range(outers):
            for q in range(PLANE):
                arrived(which, device(outer + outers - d, place + PLANE - q, 1 - core))
    for copy in started:
        copy.wait_send()
    for copy in own:
        copy.wait()


def gathered(rights, lefts, n):
    pieces = jax.ShapeDtypeStruct((n,) + rights.shape, F32)
    outers = n // (CORES * PLANE)
    vmem = pl.BlockSpec(memory_space=pltpu.VMEM)
    anywhere = pl.BlockSpec(memory_space=pl.ANY)
    dma = pltpu.SemaphoreType.DMA
    return pl.pallas_call(
        functools.partial(gather_kernel, n),
        out_shape=(pieces, pieces),
        in_specs=[vmem, vmem],
        out_specs=(anywhere, anywhere),
        scratch_shapes=[
            dma((2,)),
            dma((2, max(outers - 1, 1))),
            dma((2, outers, PLANE - 1)),
            dma((2, outers, PLANE)),
            dma((2, n)),
        ],
        compiler_params=pltpu.CompilerParams(collective_id=0, has_side_effects=True),
        name="gather",
    )(rights, lefts)


def local(n, a_band, b_band, z_band, stacked_left_factors, right_factors, starts):
    width = stacked_left_factors.shape[1]
    count = starts.shape[0]
    rows, cols = a_band.shape
    wide = width - ALIGN
    rights, lefts = gathered(right_factors, stacked_left_factors, n)
    rights = rights.reshape(count, width, width)
    lefts = lefts.reshape(count, width, width)
    first = (lax.axis_index("col") * cols).astype(jnp.int32)
    info = jnp.concatenate([starts, first[None]])
    far = cols // wide - 1
    params = pltpu.CompilerParams(vmem_limit_bytes=VMEM_LIMIT)
    all_rights = pl.BlockSpec((count, width, width), lambda *_: (0, 0, 0), pipeline_mode=pl.Buffered(1))
    strip = jax.ShapeDtypeStruct((3, rows, ALIGN), F32)
    low = pl.BlockSpec((width, wide), lambda j, s: (j, 0))
    high = pl.BlockSpec((width, wide), lambda j, s: (j, far))
    strip_spec = pl.BlockSpec((3, width, ALIGN), lambda j, *_: (0, j, 0))
    down, up = pl.pallas_call(
        functools.partial(prep_kernel, count, width, cols),
        out_shape=(strip, strip),
        grid_spec=pltpu.PrefetchScalarGridSpec(
            num_scalar_prefetch=1,
            grid=(count,),
            in_specs=[low, high, low, high, low, high, all_rights],
            out_specs=[strip_spec, strip_spec],
        ),
        compiler_params=params,
        name="prep",
    )(info, a_band, a_band, b_band, b_band, z_band, z_band, rights)
    whole = jax.ShapeDtypeStruct((rows, cols), F32)
    slab = pl.BlockSpec((width, cols), lambda j, s: (j, 0))
    one_left = pl.BlockSpec((None, width, width), lambda j, *_: (j, 0, 0))
    main = pl.pallas_call(
        functools.partial(main_kernel, count, width, cols),
        out_shape=(whole, whole, whole),
        grid_spec=pltpu.PrefetchScalarGridSpec(
            num_scalar_prefetch=1,
            grid=(count,),
            in_specs=[slab, slab, slab, one_left, all_rights],
            out_specs=[slab, slab, slab],
        ),
        compiler_params=params,
        cost_estimate=pl.CostEstimate(
            flops=20 * rows * cols * width, bytes_accessed=24 * rows * cols, transcendentals=0
        ),
        name="main",
    )

    def exchange(odd, even, up, down, *operands):
        wanted = {1: odd, 0: even}
        pairs = [
            (i, i + 1)
            for i in range(n - 1)
            if (i + 1) % CORES or wanted[(i + 1) // CORES % 2]
        ]
        from_left = lax.ppermute(up, "col", pairs)
        from_right = lax.ppermute(down, "col", [(j, i) for i, j in pairs])
        return (from_left, from_right) + tuple(main(*operands))

    crossed = (starts + (width - 1)) // cols
    chip_border = crossed % CORES == 0
    odd_ones = jnp.any(chip_border & (crossed // CORES % 2 == 1))
    even_ones = jnp.any(chip_border & (crossed // CORES % 2 == 0))
    from_left, from_right, a_mid, b_mid, z_mid = lax.switch(
        odd_ones.astype(jnp.int32) + 2 * even_ones.astype(jnp.int32),
        [functools.partial(exchange, odd, even) for even in (False, True) for odd in (False, True)],
        up, down, info, a_band, b_band, z_band, lefts, rights,
    )

    def edge(upto):
        def index(step, info):
            block, at_high = edge_of(count, width, cols, upto, step, info)
            return block, at_high * far

        return pl.BlockSpec((width, wide), index)

    edges = [edge(True), edge(True), edge(False)]
    strip_of = pl.BlockSpec((3, width, ALIGN), lambda step, s: (0, lax.rem(step, count), 0))
    left_of = pl.BlockSpec((None, width, width), lambda step, s: (lax.rem(step, count), 0, 0))
    return pl.pallas_call(
        functools.partial(finish_kernel, count, width, cols),
        out_shape=(whole, whole, whole),
        grid_spec=pltpu.PrefetchScalarGridSpec(
            num_scalar_prefetch=1,
            grid=(2 * count,),
            in_specs=edges + [strip_of, strip_of, left_of, all_rights],
            out_specs=edges,
        ),
        input_output_aliases={1: 0, 2: 1, 3: 2},
        compiler_params=params,
        name="finish",
    )(info, a_mid, b_mid, z_mid, from_left, from_right, lefts, rights)


def solution(mesh):
    placed = (P(None, "col"), P(None, "col"), P(None, "col"), P("col", None), P("col", None), P())
    return jax.shard_map(
        functools.partial(local, mesh.shape["col"]),
        mesh=mesh,
        in_specs=placed,
        out_specs=(P(None, "col"), P(None, "col"), P(None, "col")),
        check_vma=False,
    )
```

```python
import functools

import jax
import jax.numpy as jnp
from jax import lax
from jax.experimental import pallas as pl
from jax.experimental.pallas import tpu as pltpu
from jax.sharding import PartitionSpec as P

ALIGN = 128
CORES = 2
PLANE = 4
F32 = jnp.float32
BF16 = jnp.bfloat16
VMEM_LIMIT = 60 * 1024 * 1024


def split(x):
    high = x.astype(BF16)
    return high, (x - high.astype(F32)).astype(BF16)


def mm(x, w):
    rows = x.shape[0]
    xh, xl = split(x)
    wh, wl = split(w)
    both = jnp.dot(jnp.concatenate([xh, xl], axis=0), wh, preferred_element_type=F32)
    return both[:rows] + (both[rows:] + jnp.dot(xh, wl, preferred_element_type=F32))


def borders(info, count, width, cols):
    first = info[count]
    last = first + cols
    left = (jnp.bool_(False), jnp.int32(0), jnp.int32(0))
    right = left
    for k in range(count):
        s = info[k]
        at_left = (s < first) & (first < s + width)
        at_right = (s < last) & (last < s + width)
        left = (
            left[0] | at_left,
            jnp.where(at_left, k, left[1]),
            jnp.where(at_left, s + width - first, left[2]),
        )
        right = (
            right[0] | at_right,
            jnp.where(at_right, k, right[1]),
            jnp.where(at_right, last - s, right[2]),
        )
    return first, left, right


def prep_kernel(count, width, cols, info, al, ar, bl, br, zl, zr, rights, down, up):
    wide = width - ALIGN
    _, left, right = borders(info, count, width, cols)
    for i, (lo, hi) in enumerate(((al, ar), (bl, br), (zl, zr))):
        full_left = left[0] & (left[2] == wide)
        full_right = right[0] & (right[2] == wide)

        @pl.when(full_left)
        def _():
            down[i] = mm(lo[...], rights[left[1], width - wide : width, 0:ALIGN])

        @pl.when(jnp.logical_not(full_left))
        def _():
            down[i] = lo[:, 0:ALIGN]

        @pl.when(full_right)
        def _():
            up[i] = mm(hi[...], rights[right[1], 0:wide, width - ALIGN : width])

        @pl.when(jnp.logical_not(full_right))
        def _():
            up[i] = hi[:, wide - ALIGN : wide]


def main_kernel(count, width, cols, info, a, b, z, left_factor, rights, a_out, b_out, z_out):
    wide = width - ALIGN
    j = pl.program_id(0)
    first, left, right = borders(info, count, width, cols)
    threshold = info[j] - first

    @pl.when(threshold < cols)
    def _():
        turned = left_factor[...].T
        keep = lax.broadcasted_iota(jnp.int32, (width, cols), 1) >= threshold
        for src, dst in ((a, a_out), (b, b_out)):
            x = src[...]
            dst[...] = jnp.where(keep, mm(turned, x), x)

    @pl.when(threshold >= cols)
    def _():
        a_out[...] = a[...]
        b_out[...] = b[...]

    z_out[...] = z[...]
    for dst, always in ((a_out, False), (b_out, False), (z_out, True)):
        on_left = left[0] if always else left[0] & (j <= left[1])
        on_right = right[0] if always else right[0] & (j <= right[1])

        @pl.when(on_left & (left[2] == wide))
        def _():
            dst[:, 0:wide] = mm(dst[:, 0:wide], rights[left[1], width - wide : width, width - wide : width])

        @pl.when(on_left & (left[2] == ALIGN))
        def _():
            dst[:, 0:ALIGN] = mm(dst[:, 0:ALIGN], rights[left[1], width - ALIGN : width, width - ALIGN : width])

        @pl.when(on_right & (right[2] == wide))
        def _():
            dst[:, cols - wide : cols] = mm(dst[:, cols - wide : cols], rights[right[1], 0:wide, 0:wide])

        @pl.when(on_right & (right[2] == ALIGN))
        def _():
            dst[:, cols - ALIGN : cols] = mm(dst[:, cols - ALIGN : cols], rights[right[1], 0:ALIGN, 0:ALIGN])


def edge_of(count, width, cols, upto, step, info):
    _, left, right = borders(info, count, width, cols)
    side = step // count
    j = lax.rem(step, count)
    low_last, high_last = (left[1], right[1]) if upto else (count - 1, count - 1)
    low = jnp.where(left[0], jnp.where(side == 0, jnp.minimum(j, low_last), low_last), 0)
    high = jnp.where(side == 0, 0, jnp.minimum(j, high_last))
    at_high = right[0] & ((side == 1) | jnp.logical_not(left[0]))
    return jnp.where(at_high, high, low), at_high.astype(jnp.int32)


def finish_kernel(count, width, cols, info, a, b, z, from_left, from_right, left_factor, rights, a_out, b_out, z_out):
    wide = width - ALIGN
    step = pl.program_id(0)
    side = step // count
    j = lax.rem(step, count)
    _, left, right = borders(info, count, width, cols)
    for upto, group in ((True, ((a, a_out), (b, b_out))), (False, ((z, z_out),))):
        now = edge_of(count, width, cols, upto, step, info)
        then = edge_of(count, width, cols, upto, jnp.maximum(step - 1, 0), info)

        @pl.when((step == 0) | (now[0] != then[0]) | (now[1] != then[1]))
        def _():
            for src, dst in group:
                dst[...] = src[...]

    def add(received, at, rows_of, near, far, window):
        present, k, here = window
        for i, dst in enumerate((a_out, b_out, z_out)):
            wanted = present & (side == at)
            if i < 2:
                wanted = wanted & (j <= k)

            @pl.when(wanted)
            def _():
                g = received[i]
                if i < 2:
                    g = mm(left_factor[...].T, g)

                @pl.when(here == wide)
                def _():
                    dst[...] = dst[...] + mm(g, rights[k, rows_of : rows_of + ALIGN, far : far + wide])

                @pl.when(here == ALIGN)
                def _():
                    dst[:, near : near + ALIGN] = dst[:, near : near + ALIGN] + g

    add(from_left, 0, 0, 0, width - wide, left)
    add(from_right, 1, width - ALIGN, wide - ALIGN, 0, right)


def gather_kernel(n, mine, everyone, own_sem, out_sems, plane_sems, core_sems, recv_sems):
    me = lax.axis_index("col")
    core = lax.rem(me, CORES)
    chip = me // CORES
    place = lax.rem(chip, PLANE)
    outer = chip // PLANE
    outers = n // (CORES * PLANE)
    beside = place + 1 - 2 * lax.rem(place, 2)
    across = lax.rem(place + 2, PLANE)
    diagonal = PLANE - 1 - place

    def device(o, p, c):
        return (lax.rem(o, outers) * PLANE + p) * CORES + c

    far = [device(outer + d, place, core) for d in range(1, outers)]
    near = [device(outer, beside, core), device(outer, across, core)]
    twin = device(outer, place, 1 - core)

    barrier = pltpu.get_barrier_semaphore()
    for peer in far + near + [twin]:
        pl.semaphore_signal(barrier, inc=1, device_id=(peer,), device_id_type=pl.DeviceIdType.MESH)
    pl.semaphore_wait(barrier, len(far) + len(near) + 1)

    started = []

    def send(source, piece, send_sem, target):
        copy = pltpu.make_async_remote_copy(
            src_ref=source,
            dst_ref=everyone.at[piece],
            send_sem=send_sem,
            recv_sem=recv_sems.at[piece],
            device_id=(target,),
            device_id_type=pl.DeviceIdType.MESH,
        )
        copy.start()
        started.append(copy)

    def arrived(piece):
        here = everyone.at[piece]
        pltpu.make_async_copy(here, here, recv_sems.at[piece]).wait()
        return here

    def spread(source, piece, d):
        for q in range(2):
            send(source, piece, plane_sems.at[d, q], near[q])
        send(source, piece, core_sems.at[d, 0], twin)

    for d in range(1, outers):
        send(mine, me, out_sems.at[d - 1], far[d - 1])
    spread(mine, me, 0)
    own = pltpu.make_async_copy(mine, everyone.at[me], own_sem.at[0])
    own.start()
    for d in range(1, outers):
        piece = device(outer + outers - d, place, core)
        spread(arrived(piece), piece, d)
    for d in range(outers):
        origin = lax.rem(outer + outers - d, outers)
        odd = lax.rem(origin, 2)
        pieces = [device(origin, beside, core), device(origin, across, core)]
        for piece in pieces:
            arrived(piece)
        relayed = pieces[0] * (1 - odd) + pieces[1] * odd
        target = near[1] * (1 - odd) + near[0] * odd
        send(everyone.at[relayed], relayed, plane_sems.at[d, 2], target)
        for q, piece in enumerate(pieces):
            send(everyone.at[piece], piece, core_sems.at[d, 1 + q], twin)
    for d in range(outers):
        piece = device(outer + outers - d, diagonal, core)
        send(arrived(piece), piece, core_sems.at[d, 3], twin)
    for d in range(outers):
        for p in (place, beside, across, diagonal):
            arrived(device(outer + outers - d, p, 1 - core))
    for copy in started:
        copy.wait_send()
    own.wait()


def gathered(mine, n, collective_id):
    outers = n // (CORES * PLANE)
    dma = pltpu.SemaphoreType.DMA
    return pl.pallas_call(
        functools.partial(gather_kernel, n),
        out_shape=jax.ShapeDtypeStruct((n,) + mine.shape, F32),
        in_specs=[pl.BlockSpec(memory_space=pltpu.VMEM)],
        out_specs=pl.BlockSpec(memory_space=pl.ANY),
        scratch_shapes=[
            dma((1,)),
            dma((max(outers - 1, 1),)),
            dma((outers, 3)),
            dma((outers, PLANE)),
            dma((n,)),
        ],
        compiler_params=pltpu.CompilerParams(collective_id=collective_id, has_side_effects=True),
        cost_estimate=pl.CostEstimate(flops=0, bytes_accessed=16 * n * mine.size, transcendentals=0),
        name="gather",
    )(mine)


def local(n, a_band, b_band, z_band, stacked_left_factors, right_factors, starts):
    width = stacked_left_factors.shape[1]
    count = starts.shape[0]
    rows, cols = a_band.shape
    wide = width - ALIGN
    rights = gathered(right_factors, n, 0).reshape(count, width, width)
    first = (lax.axis_index("col") * cols).astype(jnp.int32)
    info = jnp.concatenate([starts, first[None]])
    far = cols // wide - 1
    params = pltpu.CompilerParams(vmem_limit_bytes=VMEM_LIMIT)
    all_rights = pl.BlockSpec((count, width, width), lambda *_: (0, 0, 0), pipeline_mode=pl.Buffered(1))
    strip = jax.ShapeDtypeStruct((3, rows, ALIGN), F32)
    low = pl.BlockSpec((width, wide), lambda j, s: (j, 0))
    high = pl.BlockSpec((width, wide), lambda j, s: (j, far))
    strip_spec = pl.BlockSpec((3, width, ALIGN), lambda j, *_: (0, j, 0))
    down, up = pl.pallas_call(
        functools.partial(prep_kernel, count, width, cols),
        out_shape=(strip, strip),
        grid_spec=pltpu.PrefetchScalarGridSpec(
            num_scalar_prefetch=1,
            grid=(count,),
            in_specs=[low, high, low, high, low, high, all_rights],
            out_specs=[strip_spec, strip_spec],
        ),
        compiler_params=params,
        name="prep",
    )(info, a_band, a_band, b_band, b_band, z_band, z_band, rights)
    whole = jax.ShapeDtypeStruct((rows, cols), F32)
    slab = pl.BlockSpec((width, cols), lambda j, s: (j, 0))
    one_left = pl.BlockSpec((None, width, width), lambda j, *_: (j, 0, 0))
    main = pl.pallas_call(
        functools.partial(main_kernel, count, width, cols),
        out_shape=(whole, whole, whole),
        grid_spec=pltpu.PrefetchScalarGridSpec(
            num_scalar_prefetch=1,
            grid=(count,),
            in_specs=[slab, slab, slab, one_left, all_rights],
            out_specs=[slab, slab, slab],
        ),
        compiler_params=params,
        cost_estimate=pl.CostEstimate(
            flops=20 * rows * cols * width, bytes_accessed=24 * rows * cols, transcendentals=0
        ),
        name="main",
    )

    def exchange(odd, even, up, down, info, a_band, b_band, z_band, piece, rights):
        wanted = {1: odd, 0: even}
        pairs = [
            (i, i + 1)
            for i in range(n - 1)
            if (i + 1) % CORES or wanted[(i + 1) // CORES % 2]
        ]
        from_left = lax.ppermute(up, "col", pairs)
        from_right = lax.ppermute(down, "col", [(j, i) for i, j in pairs])
        lefts = gathered(piece, n, 1).reshape(count, width, width)
        return (from_left, from_right, lefts) + tuple(main(info, a_band, b_band, z_band, lefts, rights))

    pattern = jnp.int32(0)
    for k in range(count):
        crossed = (starts[k] + (width - 1)) // cols
        parity = 1 + (crossed // CORES + 1) % 2
        pattern = pattern | jnp.where(crossed % CORES == 0, parity, 0)
    from_left, from_right, lefts, a_mid, b_mid, z_mid = lax.switch(
        pattern,
        [functools.partial(exchange, odd, even) for even in (False, True) for odd in (False, True)],
        up, down, info, a_band, b_band, z_band, stacked_left_factors, rights,
    )

    def edge(upto):
        def index(step, info):
            block, at_high = edge_of(count, width, cols, upto, step, info)
            return block, at_high * far

        return pl.BlockSpec((width, wide), index)

    edges = [edge(True), edge(True), edge(False)]
    strip_of = pl.BlockSpec((3, width, ALIGN), lambda step, s: (0, lax.rem(step, count), 0))
    left_of = pl.BlockSpec((None, width, width), lambda step, s: (lax.rem(step, count), 0, 0))
    return pl.pallas_call(
        functools.partial(finish_kernel, count, width, cols),
        out_shape=(whole, whole, whole),
        grid_spec=pltpu.PrefetchScalarGridSpec(
            num_scalar_prefetch=1,
            grid=(2 * count,),
            in_specs=edges + [strip_of, strip_of, left_of, all_rights],
            out_specs=edges,
        ),
        input_output_aliases={1: 0, 2: 1, 3: 2},
        compiler_params=params,
        name="finish",
    )(info, a_mid, b_mid, z_mid, from_left, from_right, lefts, rights)


def solution(mesh):
    placed = (P(None, "col"), P(None, "col"), P(None, "col"), P("col", None), P("col", None), P())
    return jax.shard_map(
        functools.partial(local, mesh.shape["col"]),
        mesh=mesh,
        in_specs=placed,
        out_specs=(P(None, "col"), P(None, "col"), P(None, "col")),
        check_vma=False,
    )
```

```python
import functools

import jax
import jax.numpy as jnp
from jax import lax
from jax.experimental import pallas as pl
from jax.experimental.pallas import tpu as pltpu
from jax.sharding import PartitionSpec as P

ALIGN = 128
CORES = 2
PLANE = 4
F32 = jnp.float32
BF16 = jnp.bfloat16
VMEM_LIMIT = 60 * 1024 * 1024


def split(x):
    high = x.astype(BF16)
    return high, (x - high.astype(F32)).astype(BF16)


def mm(x, w):
    rows = x.shape[0]
    xh, xl = split(x)
    wh, wl = split(w)
    both = jnp.dot(jnp.concatenate([xh, xl], axis=0), wh, preferred_element_type=F32)
    return both[:rows] + (both[rows:] + jnp.dot(xh, wl, preferred_element_type=F32))


def borders(info, count, width, cols):
    first = info[count]
    last = first + cols
    left = (jnp.bool_(False), jnp.int32(0), jnp.int32(0))
    right = left
    for k in range(count):
        s = info[k]
        at_left = (s < first) & (first < s + width)
        at_right = (s < last) & (last < s + width)
        left = (
            left[0] | at_left,
            jnp.where(at_left, k, left[1]),
            jnp.where(at_left, s + width - first, left[2]),
        )
        right = (
            right[0] | at_right,
            jnp.where(at_right, k, right[1]),
            jnp.where(at_right, last - s, right[2]),
        )
    return first, left, right


def prep_kernel(count, width, cols, info, al, ar, bl, br, zl, zr, rights, down, up):
    wide = width - ALIGN
    _, left, right = borders(info, count, width, cols)
    for i, (lo, hi) in enumerate(((al, ar), (bl, br), (zl, zr))):
        full_left = left[0] & (left[2] == wide)
        full_right = right[0] & (right[2] == wide)

        @pl.when(full_left)
        def _():
            down[i] = mm(lo[...], rights[left[1], width - wide : width, 0:ALIGN])

        @pl.when(jnp.logical_not(full_left))
        def _():
            down[i] = lo[:, 0:ALIGN]

        @pl.when(full_right)
        def _():
            up[i] = mm(hi[...], rights[right[1], 0:wide, width - ALIGN : width])

        @pl.when(jnp.logical_not(full_right))
        def _():
            up[i] = hi[:, wide - ALIGN : wide]


def main_kernel(count, width, cols, info, a, b, z, left_factor, rights, a_out, b_out, z_out):
    wide = width - ALIGN
    j = pl.program_id(0)
    first, left, right = borders(info, count, width, cols)
    threshold = info[j] - first

    @pl.when(threshold < cols)
    def _():
        turned = left_factor[...].T
        keep = lax.broadcasted_iota(jnp.int32, (width, cols), 1) >= threshold
        for src, dst in ((a, a_out), (b, b_out)):
            x = src[...]
            dst[...] = jnp.where(keep, mm(turned, x), x)

    @pl.when(threshold >= cols)
    def _():
        a_out[...] = a[...]
        b_out[...] = b[...]

    z_out[...] = z[...]
    for dst, always in ((a_out, False), (b_out, False), (z_out, True)):
        on_left = left[0] if always else left[0] & (j <= left[1])
        on_right = right[0] if always else right[0] & (j <= right[1])

        @pl.when(on_left & (left[2] == wide))
        def _():
            dst[:, 0:wide] = mm(dst[:, 0:wide], rights[left[1], width - wide : width, width - wide : width])

        @pl.when(on_left & (left[2] == ALIGN))
        def _():
            dst[:, 0:ALIGN] = mm(dst[:, 0:ALIGN], rights[left[1], width - ALIGN : width, width - ALIGN : width])

        @pl.when(on_right & (right[2] == wide))
        def _():
            dst[:, cols - wide : cols] = mm(dst[:, cols - wide : cols], rights[right[1], 0:wide, 0:wide])

        @pl.when(on_right & (right[2] == ALIGN))
        def _():
            dst[:, cols - ALIGN : cols] = mm(dst[:, cols - ALIGN : cols], rights[right[1], 0:ALIGN, 0:ALIGN])


def edge_of(count, width, cols, upto, step, info):
    _, left, right = borders(info, count, width, cols)
    side = step // count
    j = lax.rem(step, count)
    low_last, high_last = (left[1], right[1]) if upto else (count - 1, count - 1)
    low = jnp.where(left[0], jnp.where(side == 0, jnp.minimum(j, low_last), low_last), 0)
    high = jnp.where(side == 0, 0, jnp.minimum(j, high_last))
    at_high = right[0] & ((side == 1) | jnp.logical_not(left[0]))
    return jnp.where(at_high, high, low), at_high.astype(jnp.int32)


def finish_kernel(count, width, cols, info, a, b, z, from_left, from_right, left_factor, rights, a_out, b_out, z_out):
    wide = width - ALIGN
    step = pl.program_id(0)
    side = step // count
    j = lax.rem(step, count)
    _, left, right = borders(info, count, width, cols)
    for upto, group in ((True, ((a, a_out), (b, b_out))), (False, ((z, z_out),))):
        now = edge_of(count, width, cols, upto, step, info)
        then = edge_of(count, width, cols, upto, jnp.maximum(step - 1, 0), info)

        @pl.when((step == 0) | (now[0] != then[0]) | (now[1] != then[1]))
        def _():
            for src, dst in group:
                dst[...] = src[...]

    def add(received, at, rows_of, near, far, window):
        present, k, here = window
        for i, dst in enumerate((a_out, b_out, z_out)):
            wanted = present & (side == at)
            if i < 2:
                wanted = wanted & (j <= k)

            @pl.when(wanted)
            def _():
                g = received[i]
                if i < 2:
                    g = mm(left_factor[...].T, g)

                @pl.when(here == wide)
                def _():
                    dst[...] = dst[...] + mm(g, rights[k, rows_of : rows_of + ALIGN, far : far + wide])

                @pl.when(here == ALIGN)
                def _():
                    dst[:, near : near + ALIGN] = dst[:, near : near + ALIGN] + g

    add(from_left, 0, 0, 0, width - wide, left)
    add(from_right, 1, width - ALIGN, wide - ALIGN, 0, right)


def gather_kernel(n, rights, lefts, all_rights, all_lefts, own_sem, out_sems, plane_sems, core_sems, recv_sems):
    me = lax.axis_index("col")
    core = lax.rem(me, CORES)
    chip = me // CORES
    place = lax.rem(chip, PLANE)
    outer = chip // PLANE
    outers = n // (CORES * PLANE)
    pair = ((rights, all_rights), (lefts, all_lefts))
    beside = place + 1 - 2 * lax.rem(place, 2)
    across = lax.rem(place + 2, PLANE)
    diagonal = PLANE - 1 - place

    def device(o, p, c):
        return (lax.rem(o, outers) * PLANE + p) * CORES + c

    far = [device(outer + d, place, core) for d in range(1, outers)]
    near = [device(outer, beside, core), device(outer, across, core)]
    twin = device(outer, place, 1 - core)

    barrier = pltpu.get_barrier_semaphore()
    for peer in far + near + [twin]:
        pl.semaphore_signal(barrier, inc=1, device_id=(peer,), device_id_type=pl.DeviceIdType.MESH)
    pl.semaphore_wait(barrier, len(far) + len(near) + 1)

    started = []

    def send(which, source, piece, send_sem, target):
        copy = pltpu.make_async_remote_copy(
            src_ref=source,
            dst_ref=pair[which][1].at[piece],
            send_sem=send_sem,
            recv_sem=recv_sems.at[which, piece],
            device_id=(target,),
            device_id_type=pl.DeviceIdType.MESH,
        )
        copy.start()
        started.append(copy)

    def arrived(which, piece):
        here = pair[which][1].at[piece]
        pltpu.make_async_copy(here, here, recv_sems.at[which, piece]).wait()
        return here

    def spread(which, source, piece, d):
        for q in range(2):
            send(which, source, piece, plane_sems.at[which, d, q], near[q])
        send(which, source, piece, core_sems.at[which, d, 0], twin)

    own = []
    for which, (mine, everyone) in enumerate(pair):
        for d in range(1, outers):
            send(which, mine, me, out_sems.at[which, d - 1], far[d - 1])
        spread(which, mine, me, 0)
        own.append(pltpu.make_async_copy(mine, everyone.at[me], own_sem.at[which]))
        own[-1].start()
    for which in range(2):
        for d in range(1, outers):
            piece = device(outer + outers - d, place, core)
            spread(which, arrived(which, piece), piece, d)
    for which, (_, everyone) in enumerate(pair):
        for d in range(outers):
            origin = lax.rem(outer + outers - d, outers)
            odd = lax.rem(origin + which, 2)
            pieces = [device(origin, beside, core), device(origin, across, core)]
            for piece in pieces:
                arrived(which, piece)
            relayed = pieces[0] * (1 - odd) + pieces[1] * odd
            target = near[1] * (1 - odd) + near[0] * odd
            send(which, everyone.at[relayed], relayed, plane_sems.at[which, d, 2], target)
            for q, piece in enumerate(pieces):
                send(which, everyone.at[piece], piece, core_sems.at[which, d, 1 + q], twin)
    for which in range(2):
        for d in range(outers):
            piece = device(outer + outers - d, diagonal, core)
            send(which, arrived(which, piece), piece, core_sems.at[which, d, 3], twin)
    for which in range(2):
        for d in range(outers):
            for p in (place, beside, across, diagonal):
                arrived(which, device(outer + outers - d, p, 1 - core))
    for copy in started:
        copy.wait_send()
    for copy in own:
        copy.wait()


def gathered(rights, lefts, n):
    pieces = jax.ShapeDtypeStruct((n,) + rights.shape, F32)
    outers = n // (CORES * PLANE)
    vmem = pl.BlockSpec(memory_space=pltpu.VMEM)
    anywhere = pl.BlockSpec(memory_space=pl.ANY)
    dma = pltpu.SemaphoreType.DMA
    return pl.pallas_call(
        functools.partial(gather_kernel, n),
        out_shape=(pieces, pieces),
        in_specs=[vmem, vmem],
        out_specs=(anywhere, anywhere),
        scratch_shapes=[
            dma((2,)),
            dma((2, max(outers - 1, 1))),
            dma((2, outers, PLANE - 1)),
            dma((2, outers, PLANE)),
            dma((2, n)),
        ],
        compiler_params=pltpu.CompilerParams(collective_id=0, has_side_effects=True),
        name="gather",
    )(rights, lefts)


def local(n, a_band, b_band, z_band, stacked_left_factors, right_factors, starts):
    width = stacked_left_factors.shape[1]
    count = starts.shape[0]
    rows, cols = a_band.shape
    wide = width - ALIGN
    rights, lefts = gathered(right_factors, stacked_left_factors, n)
    rights = rights.reshape(count, width, width)
    lefts = lefts.reshape(count, width, width)
    first = (lax.axis_index("col") * cols).astype(jnp.int32)
    info = jnp.concatenate([starts, first[None]])
    far = cols // wide - 1
    params = pltpu.CompilerParams(vmem_limit_bytes=VMEM_LIMIT)
    all_rights = pl.BlockSpec((count, width, width), lambda *_: (0, 0, 0), pipeline_mode=pl.Buffered(1))
    strip = jax.ShapeDtypeStruct((3, rows, ALIGN), F32)
    low = pl.BlockSpec((width, wide), lambda j, s: (j, 0))
    high = pl.BlockSpec((width, wide), lambda j, s: (j, far))
    strip_spec = pl.BlockSpec((3, width, ALIGN), lambda j, *_: (0, j, 0))
    down, up = pl.pallas_call(
        functools.partial(prep_kernel, count, width, cols),
        out_shape=(strip, strip),
        grid_spec=pltpu.PrefetchScalarGridSpec(
            num_scalar_prefetch=1,
            grid=(count,),
            in_specs=[low, high, low, high, low, high, all_rights],
            out_specs=[strip_spec, strip_spec],
        ),
        compiler_params=params,
        name="prep",
    )(info, a_band, a_band, b_band, b_band, z_band, z_band, rights)
    whole = jax.ShapeDtypeStruct((rows, cols), F32)
    slab = pl.BlockSpec((width, cols), lambda j, s: (j, 0))
    one_left = pl.BlockSpec((None, width, width), lambda j, *_: (j, 0, 0))
    main = pl.pallas_call(
        functools.partial(main_kernel, count, width, cols),
        out_shape=(whole, whole, whole),
        grid_spec=pltpu.PrefetchScalarGridSpec(
            num_scalar_prefetch=1,
            grid=(count,),
            in_specs=[slab, slab, slab, one_left, all_rights],
            out_specs=[slab, slab, slab],
        ),
        compiler_params=params,
        cost_estimate=pl.CostEstimate(
            flops=20 * rows * cols * width, bytes_accessed=24 * rows * cols, transcendentals=0
        ),
        name="main",
    )

    def exchange(odd, even, up, down, *operands):
        wanted = {1: odd, 0: even}
        pairs = [
            (i, i + 1)
            for i in range(n - 1)
            if (i + 1) % CORES or wanted[(i + 1) // CORES % 2]
        ]
        from_left = lax.ppermute(up, "col", pairs)
        from_right = lax.ppermute(down, "col", [(j, i) for i, j in pairs])
        return (from_left, from_right) + tuple(main(*operands))

    crossed = (starts + (width - 1)) // cols
    chip_border = crossed % CORES == 0
    odd_ones = jnp.any(chip_border & (crossed // CORES % 2 == 1))
    even_ones = jnp.any(chip_border & (crossed // CORES % 2 == 0))
    from_left, from_right, a_mid, b_mid, z_mid = lax.switch(
        odd_ones.astype(jnp.int32) + 2 * even_ones.astype(jnp.int32),
        [functools.partial(exchange, odd, even) for even in (False, True) for odd in (False, True)],
        up, down, info, a_band, b_band, z_band, lefts, rights,
    )

    def edge(upto):
        def index(step, info):
            block, at_high = edge_of(count, width, cols, upto, step, info)
            return block, at_high * far

        return pl.BlockSpec((width, wide), index)

    edges = [edge(True), edge(True), edge(False)]
    strip_of = pl.BlockSpec((3, width, ALIGN), lambda step, s: (0, lax.rem(step, count), 0))
    left_of = pl.BlockSpec((None, width, width), lambda step, s: (lax.rem(step, count), 0, 0))
    return pl.pallas_call(
        functools.partial(finish_kernel, count, width, cols),
        out_shape=(whole, whole, whole),
        grid_spec=pltpu.PrefetchScalarGridSpec(
            num_scalar_prefetch=1,
            grid=(2 * count,),
            in_specs=edges + [strip_of, strip_of, left_of, all_rights],
            out_specs=edges,
        ),
        input_output_aliases={1: 0, 2: 1, 3: 2},
        compiler_params=params,
        name="finish",
    )(info, a_mid, b_mid, z_mid, from_left, from_right, lefts, rights)


def solution(mesh):
    placed = (P(None, "col"), P(None, "col"), P(None, "col"), P("col", None), P("col", None), P())
    return jax.shard_map(
        functools.partial(local, mesh.shape["col"]),
        mesh=mesh,
        in_specs=placed,
        out_specs=(P(None, "col"), P(None, "col"), P(None, "col")),
        check_vma=False,
    )
```

```python
import functools

import jax
import jax.numpy as jnp
from jax import lax
from jax.experimental import pallas as pl
from jax.experimental.pallas import tpu as pltpu
from jax.sharding import PartitionSpec as P

ALIGN = 128
CORES = 2
PLANE = 4
F32 = jnp.float32
BF16 = jnp.bfloat16
VMEM_LIMIT = 60 * 1024 * 1024


def split(x):
    high = x.astype(BF16)
    return high, (x - high.astype(F32)).astype(BF16)


def mm(x, w):
    rows = x.shape[0]
    xh, xl = split(x)
    wh, wl = split(w)
    both = jnp.dot(jnp.concatenate([xh, xl], axis=0), wh, preferred_element_type=F32)
    return both[:rows] + (both[rows:] + jnp.dot(xh, wl, preferred_element_type=F32))


def borders(info, count, width, cols):
    first = info[count]
    last = first + cols
    left = (jnp.bool_(False), jnp.int32(0), jnp.int32(0))
    right = left
    for k in range(count):
        s = info[k]
        at_left = (s < first) & (first < s + width)
        at_right = (s < last) & (last < s + width)
        left = (
            left[0] | at_left,
            jnp.where(at_left, k, left[1]),
            jnp.where(at_left, s + width - first, left[2]),
        )
        right = (
            right[0] | at_right,
            jnp.where(at_right, k, right[1]),
            jnp.where(at_right, last - s, right[2]),
        )
    return first, left, right


def prep_kernel(count, width, cols, info, al, ar, bl, br, zl, zr, rights, down, up, pattern):
    wide = width - ALIGN
    _, left, right = borders(info, count, width, cols)
    chosen = [jnp.int32(0), jnp.int32(0)]
    for k in range(count):
        crossed = (info[k] + (width - 1)) // cols
        for parity in range(2):
            hit = (crossed % CORES == 0) & (crossed // CORES % 2 == parity)
            chosen[parity] = jnp.where(hit, 1, chosen[parity])
    pattern[0] = chosen[1] + 2 * chosen[0]
    for i, (lo, hi) in enumerate(((al, ar), (bl, br), (zl, zr))):
        full_left = left[0] & (left[2] == wide)
        full_right = right[0] & (right[2] == wide)

        @pl.when(full_left)
        def _():
            down[i] = mm(lo[...], rights[left[1], width - wide : width, 0:ALIGN])

        @pl.when(jnp.logical_not(full_left))
        def _():
            down[i] = lo[:, 0:ALIGN]

        @pl.when(full_right)
        def _():
            up[i] = mm(hi[...], rights[right[1], 0:wide, width - ALIGN : width])

        @pl.when(jnp.logical_not(full_right))
        def _():
            up[i] = hi[:, wide - ALIGN : wide]


def main_kernel(count, width, cols, info, a, b, z, left_factor, rights, a_out, b_out, z_out):
    wide = width - ALIGN
    j = pl.program_id(0)
    first, left, right = borders(info, count, width, cols)
    threshold = info[j] - first

    @pl.when(threshold < cols)
    def _():
        turned = left_factor[...].T
        keep = lax.broadcasted_iota(jnp.int32, (width, cols), 1) >= threshold
        for src, dst in ((a, a_out), (b, b_out)):
            x = src[...]
            dst[...] = jnp.where(keep, mm(turned, x), x)

    @pl.when(threshold >= cols)
    def _():
        a_out[...] = a[...]
        b_out[...] = b[...]

    z_out[...] = z[...]
    for dst, always in ((a_out, False), (b_out, False), (z_out, True)):
        on_left = left[0] if always else left[0] & (j <= left[1])
        on_right = right[0] if always else right[0] & (j <= right[1])

        @pl.when(on_left & (left[2] == wide))
        def _():
            dst[:, 0:wide] = mm(dst[:, 0:wide], rights[left[1], width - wide : width, width - wide : width])

        @pl.when(on_left & (left[2] == ALIGN))
        def _():
            dst[:, 0:ALIGN] = mm(dst[:, 0:ALIGN], rights[left[1], width - ALIGN : width, width - ALIGN : width])

        @pl.when(on_right & (right[2] == wide))
        def _():
            dst[:, cols - wide : cols] = mm(dst[:, cols - wide : cols], rights[right[1], 0:wide, 0:wide])

        @pl.when(on_right & (right[2] == ALIGN))
        def _():
            dst[:, cols - ALIGN : cols] = mm(dst[:, cols - ALIGN : cols], rights[right[1], 0:ALIGN, 0:ALIGN])


def edge_of(count, width, cols, upto, step, info):
    _, left, right = borders(info, count, width, cols)
    side = step // count
    j = lax.rem(step, count)
    low_last, high_last = (left[1], right[1]) if upto else (count - 1, count - 1)
    low = jnp.where(left[0], jnp.where(side == 0, jnp.minimum(j, low_last), low_last), 0)
    high = jnp.where(side == 0, 0, jnp.minimum(j, high_last))
    at_high = right[0] & ((side == 1) | jnp.logical_not(left[0]))
    return jnp.where(at_high, high, low), at_high.astype(jnp.int32)


def finish_kernel(count, width, cols, info, a, b, z, from_left, from_right, left_factor, rights, a_out, b_out, z_out):
    wide = width - ALIGN
    step = pl.program_id(0)
    side = step // count
    j = lax.rem(step, count)
    _, left, right = borders(info, count, width, cols)
    for upto, group in ((True, ((a, a_out), (b, b_out))), (False, ((z, z_out),))):
        now = edge_of(count, width, cols, upto, step, info)
        then = edge_of(count, width, cols, upto, jnp.maximum(step - 1, 0), info)

        @pl.when((step == 0) | (now[0] != then[0]) | (now[1] != then[1]))
        def _():
            for src, dst in group:
                dst[...] = src[...]

    def add(received, at, rows_of, near, far, window):
        present, k, here = window
        for i, dst in enumerate((a_out, b_out, z_out)):
            wanted = present & (side == at)
            if i < 2:
                wanted = wanted & (j <= k)

            @pl.when(wanted)
            def _():
                g = received[i]
                if i < 2:
                    g = mm(left_factor[...].T, g)

                @pl.when(here == wide)
                def _():
                    dst[...] = dst[...] + mm(g, rights[k, rows_of : rows_of + ALIGN, far : far + wide])

                @pl.when(here == ALIGN)
                def _():
                    dst[:, near : near + ALIGN] = dst[:, near : near + ALIGN] + g

    add(from_left, 0, 0, 0, width - wide, left)
    add(from_right, 1, width - ALIGN, wide - ALIGN, 0, right)


def gather_kernel(n, rights, lefts, all_rights, all_lefts, own_sem, out_sems, plane_sems, core_sems, recv_sems):
    me = lax.axis_index("col")
    core = lax.rem(me, CORES)
    chip = me // CORES
    place = lax.rem(chip, PLANE)
    outer = chip // PLANE
    outers = n // (CORES * PLANE)
    pair = ((rights, all_rights), (lefts, all_lefts))
    beside = place + 1 - 2 * lax.rem(place, 2)
    across = lax.rem(place + 2, PLANE)
    diagonal = PLANE - 1 - place

    def device(o, p, c):
        return (lax.rem(o, outers) * PLANE + p) * CORES + c

    far = [device(outer + d, place, core) for d in range(1, outers)]
    near = [device(outer, beside, core), device(outer, across, core)]
    twin = device(outer, place, 1 - core)

    barrier = pltpu.get_barrier_semaphore()
    for peer in far + near + [twin]:
        pl.semaphore_signal(barrier, inc=1, device_id=(peer,), device_id_type=pl.DeviceIdType.MESH)
    pl.semaphore_wait(barrier, len(far) + len(near) + 1)

    started = []

    def send(which, source, piece, send_sem, target):
        copy = pltpu.make_async_remote_copy(
            src_ref=source,
            dst_ref=pair[which][1].at[piece],
            send_sem=send_sem,
            recv_sem=recv_sems.at[which, piece],
            device_id=(target,),
            device_id_type=pl.DeviceIdType.MESH,
        )
        copy.start()
        started.append(copy)

    def arrived(which, piece):
        here = pair[which][1].at[piece]
        pltpu.make_async_copy(here, here, recv_sems.at[which, piece]).wait()
        return here

    def spread(which, source, piece, d):
        for q in range(2):
            send(which, source, piece, plane_sems.at[which, d, q], near[q])
        send(which, source, piece, core_sems.at[which, d, 0], twin)

    own = []
    for which, (mine, everyone) in enumerate(pair):
        for d in range(1, outers):
            send(which, mine, me, out_sems.at[which, d - 1], far[d - 1])
        spread(which, mine, me, 0)
        own.append(pltpu.make_async_copy(mine, everyone.at[me], own_sem.at[which]))
        own[-1].start()
    for which in range(2):
        for d in range(1, outers):
            piece = device(outer + outers - d, place, core)
            spread(which, arrived(which, piece), piece, d)
    for which, (_, everyone) in enumerate(pair):
        for d in range(outers):
            origin = lax.rem(outer + outers - d, outers)
            odd = lax.rem(origin + which, 2)
            pieces = [device(origin, beside, core), device(origin, across, core)]
            for piece in pieces:
                arrived(which, piece)
            relayed = pieces[0] * (1 - odd) + pieces[1] * odd
            target = near[1] * (1 - odd) + near[0] * odd
            send(which, everyone.at[relayed], relayed, plane_sems.at[which, d, 2], target)
            for q, piece in enumerate(pieces):
                send(which, everyone.at[piece], piece, core_sems.at[which, d, 1 + q], twin)
    for which in range(2):
        for d in range(outers):
            piece = device(outer + outers - d, diagonal, core)
            send(which, arrived(which, piece), piece, core_sems.at[which, d, 3], twin)
    for which in range(2):
        for d in range(outers):
            for p in (place, beside, across, diagonal):
                arrived(which, device(outer + outers - d, p, 1 - core))
    for copy in started:
        copy.wait_send()
    for copy in own:
        copy.wait()


def gathered(rights, lefts, n):
    pieces = jax.ShapeDtypeStruct((n,) + rights.shape, F32)
    outers = n // (CORES * PLANE)
    vmem = pl.BlockSpec(memory_space=pltpu.VMEM)
    anywhere = pl.BlockSpec(memory_space=pl.ANY)
    dma = pltpu.SemaphoreType.DMA
    return pl.pallas_call(
        functools.partial(gather_kernel, n),
        out_shape=(pieces, pieces),
        in_specs=[vmem, vmem],
        out_specs=(anywhere, anywhere),
        scratch_shapes=[
            dma((2,)),
            dma((2, max(outers - 1, 1))),
            dma((2, outers, PLANE - 1)),
            dma((2, outers, PLANE)),
            dma((2, n)),
        ],
        compiler_params=pltpu.CompilerParams(collective_id=0, has_side_effects=True),
        name="gather",
    )(rights, lefts)


def local(n, a_band, b_band, z_band, stacked_left_factors, right_factors, starts):
    width = stacked_left_factors.shape[1]
    count = starts.shape[0]
    rows, cols = a_band.shape
    wide = width - ALIGN
    rights, lefts = gathered(right_factors, stacked_left_factors, n)
    rights = rights.reshape(count, width, width)
    lefts = lefts.reshape(count, width, width)
    first = (lax.axis_index("col") * cols).astype(jnp.int32)
    info = jnp.concatenate([starts, first[None]])
    far = cols // wide - 1
    params = pltpu.CompilerParams(vmem_limit_bytes=VMEM_LIMIT)
    all_rights = pl.BlockSpec((count, width, width), lambda *_: (0, 0, 0), pipeline_mode=pl.Buffered(1))
    strip = jax.ShapeDtypeStruct((3, rows, ALIGN), F32)
    low = pl.BlockSpec((width, wide), lambda j, s: (j, 0))
    high = pl.BlockSpec((width, wide), lambda j, s: (j, far))
    strip_spec = pl.BlockSpec((3, width, ALIGN), lambda j, *_: (0, j, 0))
    down, up, pattern = pl.pallas_call(
        functools.partial(prep_kernel, count, width, cols),
        out_shape=(strip, strip, jax.ShapeDtypeStruct((1,), jnp.int32)),
        grid_spec=pltpu.PrefetchScalarGridSpec(
            num_scalar_prefetch=1,
            grid=(count,),
            in_specs=[low, high, low, high, low, high, all_rights],
            out_specs=[strip_spec, strip_spec, pl.BlockSpec(memory_space=pltpu.SMEM)],
        ),
        compiler_params=params,
        name="prep",
    )(info, a_band, a_band, b_band, b_band, z_band, z_band, rights)
    whole = jax.ShapeDtypeStruct((rows, cols), F32)
    slab = pl.BlockSpec((width, cols), lambda j, s: (j, 0))
    one_left = pl.BlockSpec((None, width, width), lambda j, *_: (j, 0, 0))
    main = pl.pallas_call(
        functools.partial(main_kernel, count, width, cols),
        out_shape=(whole, whole, whole),
        grid_spec=pltpu.PrefetchScalarGridSpec(
            num_scalar_prefetch=1,
            grid=(count,),
            in_specs=[slab, slab, slab, one_left, all_rights],
            out_specs=[slab, slab, slab],
        ),
        compiler_params=params,
        cost_estimate=pl.CostEstimate(
            flops=20 * rows * cols * width, bytes_accessed=24 * rows * cols, transcendentals=0
        ),
        name="main",
    )

    def exchange(odd, even, up, down, *operands):
        wanted = {1: odd, 0: even}
        pairs = [
            (i, i + 1)
            for i in range(n - 1)
            if (i + 1) % CORES or wanted[(i + 1) // CORES % 2]
        ]
        from_left = lax.ppermute(up, "col", pairs)
        from_right = lax.ppermute(down, "col", [(j, i) for i, j in pairs])
        return (from_left, from_right) + tuple(main(*operands))

    from_left, from_right, a_mid, b_mid, z_mid = lax.switch(
        pattern[0],
        [functools.partial(exchange, odd, even) for even in (False, True) for odd in (False, True)],
        up, down, info, a_band, b_band, z_band, lefts, rights,
    )

    def edge(upto):
        def index(step, info):
            block, at_high = edge_of(count, width, cols, upto, step, info)
            return block, at_high * far

        return pl.BlockSpec((width, wide), index)

    edges = [edge(True), edge(True), edge(False)]
    strip_of = pl.BlockSpec((3, width, ALIGN), lambda step, s: (0, lax.rem(step, count), 0))
    left_of = pl.BlockSpec((None, width, width), lambda step, s: (lax.rem(step, count), 0, 0))
    return pl.pallas_call(
        functools.partial(finish_kernel, count, width, cols),
        out_shape=(whole, whole, whole),
        grid_spec=pltpu.PrefetchScalarGridSpec(
            num_scalar_prefetch=1,
            grid=(2 * count,),
            in_specs=edges + [strip_of, strip_of, left_of, all_rights],
            out_specs=edges,
        ),
        input_output_aliases={1: 0, 2: 1, 3: 2},
        compiler_params=params,
        name="finish",
    )(info, a_mid, b_mid, z_mid, from_left, from_right, lefts, rights)


def solution(mesh):
    placed = (P(None, "col"), P(None, "col"), P(None, "col"), P("col", None), P("col", None), P())
    return jax.shard_map(
        functools.partial(local, mesh.shape["col"]),
        mesh=mesh,
        in_specs=placed,
        out_specs=(P(None, "col"), P(None, "col"), P(None, "col")),
        check_vma=False,
    )
```
